32 devices in a mesh: col: 8 (over z, y), row: 4 (over x, core).
Axes of the slice: x: 2, y: 2, z: 4, core: 2. Of those that a mesh axis runs over, the one named last changes fastest.
Arguments:
- panel: float32 [2, 12288, 6144], P(None, 'row', 'col'), may hold values from -0.078125 to 0.078125
- prior: float32 [6144, 64], P('col'), may hold values from -6 to 6
- right_side: float32 [2, 12288, 64], P(None, 'row'), may hold values from -6 to 6
- coupling: float32 [12288, 12288], P('row', 'col'), may hold values from -0.0546875 to 0.0546875
- inverses: float32 [2, 12288, 12288], P(None, 'row', 'col'), as said below
Outputs:
- solved: float32 [2, 12288, 64], P(None, 'row')
The draws below stay inside these ranges and needn't reach their ends.
Inputs may be any that keep to these rules, and one draw needn't show every extreme that they name: `inverses`: each of the two blocks is zero above its diagonal, and its diagonal lies between 0.5 and 2.
All inputs are finite; a program needn't handle non-finite values.
Results may differ from the reference program's by a relative error of at most 0.00011.
Values sent between devices are 32-bit elements; how exact they have to be, the bound alone decides.
A program may use at most 128 MiB of HBM per device.

```python
import math
import jax
import jax.numpy as jnp
from jax import lax

NB = 12288
R = 64
K = 6144


def draw_inverses(key, part):
    inner = jax.random.fold_in(key, 11)
    key_below, key_diag = jax.random.split(inner)
    rows = lax.broadcasted_iota(jnp.int32, (2, NB, NB), 1)
    cols = lax.broadcasted_iota(jnp.int32, (2, NB, NB), 2)
    below = jax.random.normal(key_below, (2, NB, NB), jnp.float32) / math.sqrt(NB)
    diag = jnp.exp(jax.random.uniform(key_diag, (2, NB, 1), jnp.float32, math.log(0.5), math.log(2.0)))
    return jnp.where(rows > cols, below, jnp.where(rows == cols, diag, 0.0))


def levels(rng, extent, cuts, low, high):
    level = 1.0
    for axis_at, blocks in cuts:
        steps = jax.random.uniform(jax.random.fold_in(jax.random.fold_in(rng, 6), axis_at), (blocks,), jnp.float32, low / len(cuts), high / len(cuts))
        level = level * jnp.repeat(jnp.exp(steps), extent[axis_at] // blocks).reshape((-1,) + (1,) * (len(extent) - 1 - axis_at))
    return level


def normal_values(own_key, dims, spread, limit, pieces=(), kind=jnp.bfloat16):
    values = spread * jax.random.normal(own_key, dims, jnp.float32)
    if pieces:
        values = values * levels(own_key, dims, pieces, -0.22, 0.18)
    return jnp.clip(values, -limit, limit).astype(kind)


def setup_inputs(seed: int = 0) -> dict:
    key_list = jax.random.split(jax.random.key(seed), 6)
    return {
        "panel": normal_values(key_list[0], (2, NB, K), K ** -0.5, 0.078125, ((1, 4), (2, 8)), jnp.float32),
        "prior": normal_values(key_list[1], (K, R), 1.0, 6.0, ((0, 8),), jnp.float32),
        "right_side": normal_values(key_list[2], (2, NB, R), 1.0, 6.0, ((1, 4),), jnp.float32),
        "coupling": normal_values(key_list[3], (NB, NB), NB ** -0.5, 0.0546875, ((0, 4), (1, 8)), jnp.float32),
        "inverses": draw_inverses(jax.random.fold_in(key_list[5], 71), 0),
    }


def reference(panel, prior, right_side, coupling, inverses):
    highest = lax.Precision.HIGHEST
    carried = jnp.einsum("bik,kr->bir", panel, prior, precision=highest)
    first = right_side[0] - carried[0]
    leading = jnp.dot(inverses[0], first, precision=highest)
    second = right_side[1] - (carried[1] + jnp.dot(coupling, leading, precision=highest))
    trailing = jnp.dot(inverses[1], second, precision=highest)
    return jnp.stack([leading, trailing])
```

```python
import functools
import jax
import jax.numpy as jnp
from jax import lax
from jax.experimental import pallas as pl
from jax.experimental.pallas import tpu as pltpu
from jax.sharding import PartitionSpec as P

F32, BF16 = jnp.float32, jnp.bfloat16


def kernel(q, nr, panel, prior, rs, coup, inv, out, part, part1, ra, rb, tv, xv, wv, w0, pbuf, buf0, buf1, rsv,
           psem, sem0, sem1, rsem, a_s, a_r, b_s, b_r, c1_s, x_r, c2_s, d_s, d_r, dy_s, dy_r):
    zn = nr
    nx = nr // 2
    hp = part.shape[2]
    pr = 2 * hp
    r = prior.shape[1]
    nb = q * zn
    col = lax.axis_index("col")
    i = lax.axis_index("row")
    z, y = lax.div(col, q), lax.rem(col, q)
    low = lax.broadcasted_iota(jnp.int32, (hp, 2 * r), 1) < r
    below = z <= i
    hub = z == i
    relay = jnp.logical_and(lax.rem(i, 2) == lax.rem(z, 2), lax.div(i, 2) != lax.div(z, 2))
    sibling = i + 1 - 2 * lax.rem(i, 2)

    def dev(zz, yy, ii):
        return {"col": zz * q + yy, "row": ii}

    def zfwd(k):
        return lax.rem(z + 1 + k, zn)

    def zback(k):
        return lax.rem(z + zn - 1 - k, zn)

    def yfwd(m):
        return lax.rem(y + 1 + m, q)

    def yback(m):
        return lax.rem(y + q - 1 - m, q)

    def remote(src, dst, ss, rr, to):
        return pltpu.make_async_remote_copy(
            src_ref=src, dst_ref=dst, send_sem=ss, recv_sem=rr, device_id=to, device_id_type=pl.DeviceIdType.MESH)

    def rows_of(m, k):
        return pl.ds(pl.multiple_of((yfwd(m) * zn + zfwd(k)) * pr, pr), pr)

    def load(src, dst, sem, m, k):
        rows = rows_of(m, k)
        return pltpu.make_async_copy(src.at[rows, :], dst.at[rows, :], sem.at[m * zn + k])

    def load_all(src, dst, sem):
        for m in range(q):
            pl.loop(0, zn)(lambda k, m=m: load(src, dst, sem, m, k).start())

    load_all(panel.at[0], pbuf, psem)
    mine = pl.ds(pl.multiple_of((y * zn + z) * pr, pr), pr)
    rs_copies = [pltpu.make_async_copy(rs.at[b, mine, :], rsv.at[b], rsem.at[b]) for b in range(2)]
    for c in rs_copies:
        c.start()
    pl.when(below)(lambda: load_all(inv.at[0], buf0, sem0))

    barrier = pltpu.get_barrier_semaphore()
    for k in range(zn - 1):
        pl.semaphore_signal(barrier, inc=1, device_id=dev(zfwd(k), y, i), device_id_type=pl.DeviceIdType.MESH)
    for m in range(q - 1):
        pl.semaphore_signal(barrier, inc=1, device_id=dev(z, yfwd(m), i), device_id_type=pl.DeviceIdType.MESH)
    for n in range(nr - 1):
        pl.semaphore_signal(barrier, inc=1, device_id=dev(z, y, lax.rem(i + 1 + n, nr)), device_id_type=pl.DeviceIdType.MESH)

    def split(d):
        n = d.shape[0]
        lo = lax.broadcasted_iota(jnp.int32, (n, 2 * r), 1) < r
        return jnp.where(lo, d, d - d.astype(BF16).astype(F32)).astype(BF16)

    v = prior[...]
    w0[...] = split(jnp.concatenate([v, v], axis=1))
    for c in rs_copies:
        c.wait()

    def base(b):
        return jnp.concatenate([rsv[b, :hp, :], rsv[b, hp:, :]], axis=1)

    pl.semaphore_wait(barrier, zn - 1 + q - 1 + nr - 1)

    def product(buf, w, m, k):
        a = buf[rows_of(m, k), :]
        a1 = a.astype(BF16)
        a2 = (a - a1.astype(F32)).astype(BF16)
        p = jnp.dot(jnp.concatenate([a1, a2], axis=0), w[...], preferred_element_type=F32)
        s = p[:pr] + p[pr:]
        s = s + pltpu.roll(s, r, 1)
        return jnp.where(low, s[:hp], s[hp:])

    def a_copy(ph, m, k):
        return remote(part.at[yfwd(m), zfwd(k)], ra.at[ph, m, k], a_s.at[ph, m, k], a_r.at[ph, m, k], dev(z, yfwd(m), i))

    def b_copy(ph, k):
        return remote(part.at[y, zfwd(k)], rb.at[ph, k], b_s.at[ph, k], b_r.at[ph, k], dev(zfwd(k), y, i))

    def guard(tri, cond, f):
        if tri:
            pl.when(cond)(f)
        else:
            f()

    def reduce(ph, src, buf, sem, w, tri, rhs, add=False, after=None, middle=None):
        def compute():
            for m in range(q):
                @pl.loop(0, zn)
                def _(k):
                    load(src, buf, sem, m, k).wait()
                    val = product(buf, w, m, k)
                    if add:
                        val = val + part1[yfwd(m), zfwd(k)]
                    part[yfwd(m), zfwd(k)] = val
                    if m < q - 1:
                        a_copy(ph, m, k).start()
                    if after is not None:
                        load(after, buf, sem, m, k).start()

        guard(tri, below, compute)
        if middle is not None:
            middle()

        def collect():
            def one(k):
                val = part[y, zfwd(k)]
                for m in range(q - 1):
                    a_copy(ph, m, k).wait_recv()
                    val = val + ra[ph, m, k]
                part[y, zfwd(k)] = val

            @pl.loop(0, zn - 1)
            def _(k):
                one(k)
                b_copy(ph, k).start()

            one(zn - 1)

        guard(tri, below, collect)
        if tri:
            @pl.when(jnp.logical_not(below))
            def _():
                part[y, z] = jnp.zeros((hp, 2 * r), F32)
        for k in range(zn - 1):
            def take(k=k):
                b_copy(ph, k).wait_recv()
                part[y, z] = part[y, z] + rb[ph, k]

            guard(tri, zback(k) <= i, take)
        tv[ph] = part[y, z] if rhs is None else base(rhs) - part[y, z]

    def drain(ph, tri):
        def waits():
            for m in range(q - 1):
                pl.loop(0, zn)(lambda k, m=m: a_copy(ph, m, k).wait_send())
            pl.loop(0, zn - 1)(lambda k: b_copy(ph, k).wait_send())

        guard(tri, below, waits)

    def spread(ph):
        up = remote(tv.at[ph], xv.at[ph, z], c1_s.at[ph], x_r.at[ph, z], dev(i, y, i))

        def fwd(s, n):
            to = sibling if n == 0 else lax.rem(i + 2 * n, nr)
            return remote(xv.at[ph, s], xv.at[ph, s], c2_s.at[ph, s, n], x_r.at[ph, s], dev(z, y, to))

        @pl.when(hub)
        def _():
            xv[ph, z] = tv[ph]

        pl.when(jnp.logical_not(hub))(lambda: up.start())

        @pl.loop(0, zn)
        def _(k):
            s = lax.rem(z + k, zn)
            pl.when(jnp.logical_not(jnp.logical_and(hub, s == z)))(lambda: fwd(s, 0).wait_recv())

            @pl.when(hub)
            def _():
                for n in range(1, nx):
                    fwd(s, n).start()
                fwd(s, 0).start()

            pl.when(relay)(lambda: fwd(s, 0).start())
            u = xv[ph, s]
            ur = pltpu.roll(u, r, 1)
            at = pl.multiple_of(s * pr, pr)
            wv[pl.ds(at, pr), :] = jnp.concatenate(
                [split(jnp.where(low, u, ur)), split(jnp.where(low, ur, u))], axis=0)

        def finish():
            pl.when(jnp.logical_not(hub))(lambda: up.wait_send())

            @pl.when(hub)
            def _():
                @pl.loop(0, zn)
                def _(s):
                    for n in range(nx):
                        fwd(s, n).wait_send()

            @pl.when(relay)
            def _():
                pl.loop(0, zn)(lambda s: fwd(s, 0).wait_send())

        return finish

    def dz_copy(b, ph, k):
        return remote(tv.at[ph], out.at[b, y, z], d_s.at[b, k], d_r.at[b, k], dev(zfwd(k), y, i))

    def dy_copy(b, m, slot, s):
        return remote(out.at[b, y, s], out.at[b, y, s], dy_s.at[b, m, slot], dy_r.at[b, m, slot], dev(z, yfwd(m), i))

    def publish_z(b, ph):
        out[b, y, z] = tv[ph]
        for k in range(zn - 1):
            dz_copy(b, ph, k).start()

    def publish_y(b, ph):
        for m in range(q - 1):
            dy_copy(b, m, 0, z).start()
        for k in range(zn - 1):
            remote(tv.at[ph], out.at[b, y, zback(k)], d_s.at[b, k], d_r.at[b, k], dev(zfwd(k), y, i)).wait_recv()
            for m in range(q - 1):
                dy_copy(b, m, k + 1, zback(k)).start()

    def publish_end(b, ph):
        for slot in range(zn):
            s = z if slot == 0 else zback(slot - 1)
            for m in range(q - 1):
                there = out.at[b, yback(m), s]
                remote(there, there, dy_s.at[b, m, slot], dy_r.at[b, m, slot], dev(z, yfwd(m), i)).wait_recv()
                dy_copy(b, m, slot, s).wait_send()
        for k in range(zn - 1):
            dz_copy(b, ph, k).wait_send()

    def second_carried():
        for m in range(q):
            @pl.loop(0, zn)
            def _(k):
                load(panel.at[1], pbuf, psem, m, k).wait()
                part1[yfwd(m), zfwd(k)] = product(pbuf, w0, m, k)

    reduce(0, panel.at[0], pbuf, psem, w0, False, 0, after=panel.at[1], middle=second_carried)
    load_all(coup, buf1, sem1)
    end0 = spread(0)
    drain(0, False)
    reduce(1, inv.at[0], buf0, sem0, wv, True, None, after=inv.at[1])
    end1 = spread(1)
    drain(1, True)
    publish_z(0, 1)
    reduce(2, coup, buf1, sem1, wv, False, 1, add=True)
    end2 = spread(2)
    drain(2, False)
    publish_y(0, 1)
    reduce(3, inv.at[1], buf0, sem0, wv, True, None)
    publish_z(1, 3)
    publish_y(1, 3)
    drain(3, True)
    end0()
    end1()
    end2()
    publish_end(0, 1)
    publish_end(1, 3)


def shards(nc, nr, panel, prior, right_side, coupling, inverses):
    q = nc // nr
    rows, width = coupling.shape
    r = prior.shape[1]
    hp = rows // (q * nr * 2)
    lanes = 2 * r
    dma = pltpu.SemaphoreType.DMA
    hbm = pl.BlockSpec(memory_space=pl.ANY)
    vmem = pl.BlockSpec(memory_space=pltpu.VMEM)
    packed = pl.pallas_call(
        functools.partial(kernel, q, nr),
        out_shape=jax.ShapeDtypeStruct((2, q, nr, hp, lanes), F32),
        in_specs=[hbm, vmem, hbm, hbm, hbm],
        out_specs=vmem,
        scratch_shapes=[
            pltpu.VMEM((q, nr, hp, lanes), F32),
            pltpu.VMEM((q, nr, hp, lanes), F32),
            pltpu.VMEM((4, q - 1, nr, hp, lanes), F32),
            pltpu.VMEM((4, nr - 1, hp, lanes), F32),
            pltpu.VMEM((4, hp, lanes), F32),
            pltpu.VMEM((3, nr, hp, lanes), F32),
            pltpu.VMEM((width, lanes), BF16),
            pltpu.VMEM((prior.shape[0], lanes), BF16),
            pltpu.VMEM(panel.shape[1:], F32),
            pltpu.VMEM((rows, width), F32),
            pltpu.VMEM((rows, width), F32),
            pltpu.VMEM((2, 2 * hp, r), F32),
            dma((nc,)), dma((nc,)), dma((nc,)), dma((2,)),
            dma((4, q - 1, nr)), dma((4, q - 1, nr)),
            dma((4, nr - 1)), dma((4, nr - 1)),
            dma((3,)), dma((3, nr)), dma((3, nr, nr // 2)),
            dma((2, nr - 1)), dma((2, nr - 1)),
            dma((2, q - 1, nr)), dma((2, q - 1, nr)),
        ],
        compiler_params=pltpu.CompilerParams(collective_id=0, has_side_effects=True, vmem_limit_bytes=67043328),
    )(panel, prior, right_side, coupling, inverses)
    whole = packed.reshape(2, nc, hp, 2, r).transpose(0, 1, 3, 2, 4)
    return whole.reshape(2, rows, r)


def solution(mesh):
    in_specs = (
        P(None, "row", "col"),
        P("col", None),
        P(None, "row", None),
        P("row", "col"),
        P(None, "row", "col"),
    )
    out_specs = P(None, "row", None)
    body = functools.partial(shards, mesh.shape["col"], mesh.shape["row"])
    return jax.shard_map(body, mesh=mesh, in_specs=in_specs, out_specs=out_specs, check_vma=False)
```

```python
import functools
import jax
import jax.numpy as jnp
from jax import lax
from jax.experimental import pallas as pl
from jax.experimental.pallas import tpu as pltpu
from jax.sharding import PartitionSpec as P

F32, BF16 = jnp.float32, jnp.bfloat16


def kernel(q, nr, panel, prior, rs, coup, inv, out, part, part1, ra, rb, tv, xv, wv, w0, pbuf, buf0, buf1, rsv,
           psem, sem0, sem1, rsem, a_s, a_r, b_s, b_r, c1_s, x_r, c2_s, d_s, d_r, dy_s, dy_r):
    zn = nr
    nx = nr // 2
    r, pr = part.shape[2:]
    col = lax.axis_index("col")
    i = lax.axis_index("row")
    z, y = lax.div(col, q), lax.rem(col, q)
    below = z <= i
    hub = z == i
    direct = lax.rem(i, 2) == lax.rem(z, 2)
    far = jnp.logical_and(direct, jnp.logical_not(hub))
    sibling = i + 1 - 2 * lax.rem(i, 2)

    def dev(zz, yy, ii):
        return {"col": zz * q + yy, "row": ii}

    def zfwd(k):
        return lax.rem(z + 1 + k, zn)

    def zback(k):
        return lax.rem(z + zn - 1 - k, zn)

    def yfwd(m):
        return lax.rem(y + 1 + m, q)

    def yback(m):
        return lax.rem(y + q - 1 - m, q)

    def remote(src, dst, ss, rr, to):
        return pltpu.make_async_remote_copy(
            src_ref=src, dst_ref=dst, send_sem=ss, recv_sem=rr, device_id=to, device_id_type=pl.DeviceIdType.MESH)

    def rows_of(m, k):
        return pl.ds(pl.multiple_of((yfwd(m) * zn + zfwd(k)) * pr, pr), pr)

    def load(src, dst, sem, m, k):
        rows = rows_of(m, k)
        return pltpu.make_async_copy(src.at[rows, :], dst.at[rows, :], sem.at[m * zn + k])

    def load_all(src, dst, sem):
        for m in range(q):
            pl.loop(0, zn)(lambda k, m=m: load(src, dst, sem, m, k).start())

    load_all(panel.at[0], pbuf, psem)

    def piece(ref, b, yy, zz):
        if len(ref.shape) == 4:
            return ref.at[b, yy * zn + zz]
        return ref.at[b, :, pl.ds(pl.multiple_of((yy * zn + zz) * pr, pr), pr)]

    rs_copies = [pltpu.make_async_copy(piece(rs, b, y, z), rsv.at[b], rsem.at[b]) for b in range(2)]
    for c in rs_copies:
        c.start()
    pl.when(below)(lambda: load_all(inv.at[0], buf0, sem0))

    barrier = pltpu.get_barrier_semaphore()
    for k in range(zn - 1):
        pl.semaphore_signal(barrier, inc=1, device_id=dev(zfwd(k), y, i), device_id_type=pl.DeviceIdType.MESH)
    for m in range(q - 1):
        pl.semaphore_signal(barrier, inc=1, device_id=dev(z, yfwd(m), i), device_id_type=pl.DeviceIdType.MESH)
    for n in range(nr - 1):
        pl.semaphore_signal(barrier, inc=1, device_id=dev(z, y, lax.rem(i + 1 + n, nr)), device_id_type=pl.DeviceIdType.MESH)

    @pl.when(far)
    def _():
        for k in range(zn):
            pl.semaphore_signal(barrier, inc=1, device_id=dev(k, y, z), device_id_type=pl.DeviceIdType.MESH)

    def split(x):
        high = x.astype(BF16).astype(F32)
        return jnp.concatenate([high, x - high], axis=0).T.astype(BF16)

    w0[...] = split(prior[...])
    for c in rs_copies:
        c.wait()
    pl.semaphore_wait(barrier, zn - 1 + q - 1 + nr - 1 + nx - 1)

    def product(buf, w, m, k):
        a = buf[rows_of(m, k), :]
        a1 = a.astype(BF16)
        a2 = (a - a1.astype(F32)).astype(BF16)
        p = jnp.dot(jnp.concatenate([a1, a2], axis=0), w[...], preferred_element_type=F32)
        s = (p[:pr] + p[pr:]).T
        return s[:r] + s[r:]

    def a_copy(ph, m, k):
        return remote(part.at[yfwd(m), zfwd(k)], ra.at[ph, m, k], a_s.at[ph, m, k], a_r.at[ph, m, k], dev(z, yfwd(m), i))

    def b_copy(ph, k):
        return remote(part.at[y, zfwd(k)], rb.at[ph, k], b_s.at[ph, k], b_r.at[ph, k], dev(zfwd(k), y, i))

    def guard(tri, cond, f):
        if tri:
            pl.when(cond)(f)
        else:
            f()

    def reduce(ph, src, buf, sem, w, tri, rhs, add=False, after=None, middle=None):
        def compute():
            for m in range(q):
                @pl.loop(0, zn)
                def _(k):
                    load(src, buf, sem, m, k).wait()
                    val = product(buf, w, m, k)
                    if add:
                        val = val + part1[yfwd(m), zfwd(k)]
                    part[yfwd(m), zfwd(k)] = val
                    if m < q - 1:
                        a_copy(ph, m, k).start()
                    if after is not None:
                        load(after, buf, sem, m, k).start()

        guard(tri, below, compute)
        if middle is not None:
            middle()

        def collect():
            def one(k):
                val = part[y, zfwd(k)]
                for m in range(q - 1):
                    a_copy(ph, m, k).wait_recv()
                    val = val + ra[ph, m, k]
                part[y, zfwd(k)] = val

            @pl.loop(0, zn - 1)
            def _(k):
                one(k)
                b_copy(ph, k).start()

            one(zn - 1)

        guard(tri, below, collect)
        if tri:
            @pl.when(jnp.logical_not(below))
            def _():
                part[y, z] = jnp.zeros((r, pr), F32)
        for k in range(zn - 1):
            def take(k=k):
                b_copy(ph, k).wait_recv()
                part[y, z] = part[y, z] + rb[ph, k]

            guard(tri, zback(k) <= i, take)
        tv[ph] = part[y, z] if rhs is None else rsv[rhs] - part[y, z]

    def drain(ph, tri):
        def waits():
            for m in range(q - 1):
                pl.loop(0, zn)(lambda k, m=m: a_copy(ph, m, k).wait_send())
            pl.loop(0, zn - 1)(lambda k: b_copy(ph, k).wait_send())

        guard(tri, below, waits)

    def spread(ph):
        def up(n):
            return remote(tv.at[ph], xv.at[ph, z], c1_s.at[ph, n], x_r.at[ph, z], dev(i, y, lax.rem(i + 2 * n, nr)))

        def fwd(s):
            return remote(xv.at[ph, s], xv.at[ph, s], c2_s.at[ph, s], x_r.at[ph, s], dev(z, y, sibling))

        @pl.when(hub)
        def _():
            xv[ph, z] = tv[ph]

        for n in range(1, nx):
            up(n).start()
        pl.when(jnp.logical_not(hub))(lambda: up(0).start())

        @pl.loop(0, zn)
        def _(k):
            s = lax.rem(z + k, zn)
            pl.when(jnp.logical_not(jnp.logical_and(hub, s == z)))(lambda: fwd(s).wait_recv())
            pl.when(direct)(lambda: fwd(s).start())
            wv[pl.ds(pl.multiple_of(s * pr, pr), pr), :] = split(xv[ph, s])

        def finish():
            for n in range(1, nx):
                up(n).wait_send()
            pl.when(jnp.logical_not(hub))(lambda: up(0).wait_send())
            pl.when(direct)(lambda: pl.loop(0, zn)(lambda s: fwd(s).wait_send()))

        return finish

    def dz_copy(b, ph, k):
        return remote(tv.at[ph], piece(out, b, y, z), d_s.at[b, k], d_r.at[b, k], dev(zfwd(k), y, i))

    def dy_copy(b, m, slot, s):
        return remote(piece(out, b, y, s), piece(out, b, y, s), dy_s.at[b, m, slot], dy_r.at[b, m, slot], dev(z, yfwd(m), i))

    def publish_z(b, ph):
        piece(out, b, y, z)[...] = tv[ph]
        for k in range(zn - 1):
            dz_copy(b, ph, k).start()

    def publish_y(b, ph):
        for m in range(q - 1):
            dy_copy(b, m, 0, z).start()
        for k in range(zn - 1):
            remote(tv.at[ph], piece(out, b, y, zback(k)), d_s.at[b, k], d_r.at[b, k], dev(zfwd(k), y, i)).wait_recv()
            for m in range(q - 1):
                dy_copy(b, m, k + 1, zback(k)).start()

    def publish_end(b, ph):
        for slot in range(zn):
            s = z if slot == 0 else zback(slot - 1)
            for m in range(q - 1):
                there = piece(out, b, yback(m), s)
                remote(there, there, dy_s.at[b, m, slot], dy_r.at[b, m, slot], dev(z, yfwd(m), i)).wait_recv()
                dy_copy(b, m, slot, s).wait_send()
        for k in range(zn - 1):
            dz_copy(b, ph, k).wait_send()

    def second_carried():
        for m in range(q):
            @pl.loop(0, zn)
            def _(k):
                load(panel.at[1], pbuf, psem, m, k).wait()
                part1[yfwd(m), zfwd(k)] = product(pbuf, w0, m, k)

    reduce(0, panel.at[0], pbuf, psem, w0, False, 0, after=panel.at[1], middle=second_carried)
    load_all(coup, buf1, sem1)
    end0 = spread(0)
    drain(0, False)
    reduce(1, inv.at[0], buf0, sem0, wv, True, None, after=inv.at[1])
    end1 = spread(1)
    drain(1, True)
    publish_z(0, 1)
    reduce(2, coup, buf1, sem1, wv, False, 1, add=True)
    end2 = spread(2)
    drain(2, False)
    publish_y(0, 1)
    reduce(3, inv.at[1], buf0, sem0, wv, True, None)
    publish_z(1, 3)
    publish_y(1, 3)
    drain(3, True)
    end0()
    end1()
    end2()
    publish_end(0, 1)
    publish_end(1, 3)


def shards(nc, nr, panel, prior, right_side, coupling, inverses):
    q = nc // nr
    rows, width = coupling.shape
    r = prior.shape[1]
    pr = rows // nc
    dense = pr % 128 == 0
    lanes = 2 * r
    dma = pltpu.SemaphoreType.DMA
    hbm = pl.BlockSpec(memory_space=pl.ANY)
    vmem = pl.BlockSpec(memory_space=pltpu.VMEM)
    side = right_side.transpose(0, 2, 1)
    if not dense:
        side = side.reshape(2, r, nc, pr).transpose(0, 2, 1, 3)
    solved = pl.pallas_call(
        functools.partial(kernel, q, nr),
        out_shape=jax.ShapeDtypeStruct(side.shape, F32),
        in_specs=[hbm, vmem, hbm, hbm, hbm],
        out_specs=vmem,
        scratch_shapes=[
            pltpu.VMEM((q, nr, r, pr), F32),
            pltpu.VMEM((q, nr, r, pr), F32),
            pltpu.VMEM((4, q - 1, nr, r, pr), F32),
            pltpu.VMEM((4, nr - 1, r, pr), F32),
            pltpu.VMEM((4, r, pr), F32),
            pltpu.VMEM((3, nr, r, pr), F32),
            pltpu.VMEM((width, lanes), BF16),
            pltpu.VMEM((prior.shape[0], lanes), BF16),
            pltpu.VMEM(panel.shape[1:], F32),
            pltpu.VMEM((rows, width), F32),
            pltpu.VMEM((rows, width), F32),
            pltpu.VMEM((2, r, pr), F32),
            dma((nc,)), dma((nc,)), dma((nc,)), dma((2,)),
            dma((4, q - 1, nr)), dma((4, q - 1, nr)),
            dma((4, nr - 1)), dma((4, nr - 1)),
            dma((3, nr // 2)), dma((3, nr)), dma((3, nr)),
            dma((2, nr - 1)), dma((2, nr - 1)),
            dma((2, q - 1, nr)), dma((2, q - 1, nr)),
        ],
        compiler_params=pltpu.CompilerParams(collective_id=0, has_side_effects=True, vmem_limit_bytes=67043328),
    )(panel, prior.T, side, coupling, inverses)
    if not dense:
        solved = solved.transpose(0, 2, 1, 3).reshape(2, r, rows)
    return solved.transpose(0, 2, 1)


def solution(mesh):
    in_specs = (
        P(None, "row", "col"),
        P("col", None),
        P(None, "row", None),
        P("row", "col"),
        P(None, "row", "col"),
    )
    out_specs = P(None, "row", None)
    body = functools.partial(shards, mesh.shape["col"], mesh.shape["row"])
    return jax.shard_map(body, mesh=mesh, in_specs=in_specs, out_specs=out_specs, check_vma=False)
```

```python
import functools
import jax
import jax.numpy as jnp
from jax import lax
from jax.experimental import pallas as pl
from jax.experimental.pallas import tpu as pltpu
from jax.sharding import PartitionSpec as P

F32, BF16 = jnp.float32, jnp.bfloat16
SUBS = 2


def kernel(q, nr, panel, prior, rs, coup, inv, out, part, part1, ra, rb, tv, xv, wv, w0, pbuf, buf0, buf1, rsv,
           psem, sem0, sem1, rsem, a_s, a_r, b_s, b_r, c1_s, x_r, c2_s, d_s, d_r, dy_s, dy_r):
    zn = nr
    nx = nr // 2
    r, pr = part.shape[2:]
    subs = range(SUBS)
    sub = [pl.ds(h * (r // SUBS), r // SUBS) for h in subs]
    col = lax.axis_index("col")
    i = lax.axis_index("row")
    z, y = lax.div(col, q), lax.rem(col, q)
    below = z <= i
    hub = z == i
    direct = lax.rem(i, 2) == lax.rem(z, 2)
    far = jnp.logical_and(direct, jnp.logical_not(hub))
    sibling = i + 1 - 2 * lax.rem(i, 2)

    def dev(zz, yy, ii):
        return {"col": zz * q + yy, "row": ii}

    def zfwd(k):
        return lax.rem(z + 1 + k, zn)

    def zback(k):
        return lax.rem(z + zn - 1 - k, zn)

    def yfwd(m):
        return lax.rem(y + 1 + m, q)

    def yback(m):
        return lax.rem(y + q - 1 - m, q)

    def remote(src, dst, ss, rr, to):
        return pltpu.make_async_remote_copy(
            src_ref=src, dst_ref=dst, send_sem=ss, recv_sem=rr, device_id=to, device_id_type=pl.DeviceIdType.MESH)

    def rows_of(m, k):
        return pl.ds(pl.multiple_of((yfwd(m) * zn + zfwd(k)) * pr, pr), pr)

    def load(src, dst, sem, m, k):
        rows = rows_of(m, k)
        return pltpu.make_async_copy(src.at[rows, :], dst.at[rows, :], sem.at[m * zn + k])

    def load_all(src, dst, sem):
        for m in range(q):
            pl.loop(0, zn)(lambda k, m=m: load(src, dst, sem, m, k).start())

    load_all(panel.at[0], pbuf, psem)

    def piece(ref, b, yy, zz):
        if len(ref.shape) == 4:
            return ref.at[b, yy * zn + zz]
        return ref.at[b, :, pl.ds(pl.multiple_of((yy * zn + zz) * pr, pr), pr)]

    rs_copies = [pltpu.make_async_copy(piece(rs, b, y, z), rsv.at[b], rsem.at[b]) for b in range(2)]
    for c in rs_copies:
        c.start()
    pl.when(below)(lambda: load_all(inv.at[0], buf0, sem0))

    barrier = pltpu.get_barrier_semaphore()
    for k in range(zn - 1):
        pl.semaphore_signal(barrier, inc=1, device_id=dev(zfwd(k), y, i), device_id_type=pl.DeviceIdType.MESH)
    for m in range(q - 1):
        pl.semaphore_signal(barrier, inc=1, device_id=dev(z, yfwd(m), i), device_id_type=pl.DeviceIdType.MESH)
    for n in range(nr - 1):
        pl.semaphore_signal(barrier, inc=1, device_id=dev(z, y, lax.rem(i + 1 + n, nr)), device_id_type=pl.DeviceIdType.MESH)

    @pl.when(far)
    def _():
        for k in range(zn):
            pl.semaphore_signal(barrier, inc=1, device_id=dev(k, y, z), device_id_type=pl.DeviceIdType.MESH)

    def split(x):
        high = x.astype(BF16).astype(F32)
        return jnp.concatenate([high, x - high], axis=0).T.astype(BF16)

    w0[...] = split(prior[...])
    for c in rs_copies:
        c.wait()
    pl.semaphore_wait(barrier, zn - 1 + q - 1 + nr - 1 + nx - 1)

    def product(buf, w, m, k):
        a = buf[rows_of(m, k), :]
        a1 = a.astype(BF16)
        a2 = (a - a1.astype(F32)).astype(BF16)
        p = jnp.dot(jnp.concatenate([a1, a2], axis=0), w[...], preferred_element_type=F32)
        s = (p[:pr] + p[pr:]).T
        return s[:r] + s[r:]

    def a_copy(ph, m, k, h):
        return remote(part.at[yfwd(m), zfwd(k), sub[h]], ra.at[ph, m, k, sub[h]], a_s.at[ph, m, k, h],
                      a_r.at[ph, m, k, h], dev(z, yfwd(m), i))

    def b_copy(ph, k, h):
        return remote(part.at[y, zfwd(k), sub[h]], rb.at[ph, k, sub[h]], b_s.at[ph, k, h], b_r.at[ph, k, h],
                      dev(zfwd(k), y, i))

    def guard(tri, cond, f):
        if tri:
            pl.when(cond)(f)
        else:
            f()

    def reduce(ph, src, buf, sem, w, tri, rhs, emit, add=False, after=None):
        def absorb(k, h):
            val = part[y, zfwd(k), sub[h]]
            for m in range(q - 1):
                a_copy(ph, m, k, h).wait_recv()
                val = val + ra[ph, m, k, sub[h]]
            part[y, zfwd(k), sub[h]] = val
            pl.when(k < zn - 1)(lambda: b_copy(ph, k, h).start())

        def compute():
            for m in range(q):
                @pl.loop(0, zn)
                def _(k):
                    load(src, buf, sem, m, k).wait()
                    val = product(buf, w, m, k)
                    if add:
                        val = val + part1[yfwd(m), zfwd(k)]
                    part[yfwd(m), zfwd(k)] = val
                    if after is not None:
                        load(after, buf, sem, m, k).start()
                    if m < q - 1:
                        a_copy(ph, m, k, 0).start()
                    else:
                        absorb(k, 0)

                if m < q - 1:
                    for h in subs[1:]:
                        pl.loop(0, zn)(lambda k, m=m, h=h: a_copy(ph, m, k, h).start())
            for h in subs[1:]:
                pl.loop(0, zn)(lambda k, h=h: absorb(k, h))

        guard(tri, below, compute)
        if tri:
            @pl.when(jnp.logical_not(below))
            def _():
                part[y, z] = jnp.zeros((r, pr), F32)
        for h in subs:
            for k in range(zn - 1):
                def take(k=k):
                    b_copy(ph, k, h).wait_recv()
                    part[y, z, sub[h]] = part[y, z, sub[h]] + rb[ph, k, sub[h]]

                guard(tri, zback(k) <= i, take)
            val = part[y, z, sub[h]]
            tv[ph, sub[h]] = val if rhs is None else rsv[rhs, sub[h]] - val
            emit(ph, h)

    def drain(ph, tri):
        def waits():
            for h in subs:
                for m in range(q - 1):
                    pl.loop(0, zn)(lambda k, m=m: a_copy(ph, m, k, h).wait_send())
                pl.loop(0, zn - 1)(lambda k: b_copy(ph, k, h).wait_send())

        guard(tri, below, waits)

    def up(ph, n, h):
        return remote(tv.at[ph, sub[h]], xv.at[ph, z, sub[h]], c1_s.at[ph, n, h], x_r.at[ph, z, h],
                      dev(i, y, lax.rem(i + 2 * n, nr)))

    def fwd(ph, s, h):
        there = xv.at[ph, s, sub[h]]
        return remote(there, there, c2_s.at[ph, s, h], x_r.at[ph, s, h], dev(z, y, sibling))

    def rise(ph, h):
        @pl.when(hub)
        def _():
            xv[ph, z, sub[h]] = tv[ph, sub[h]]

        for n in range(1, nx):
            up(ph, n, h).start()
        pl.when(jnp.logical_not(hub))(lambda: up(ph, 0, h).start())

    def spread(ph):
        for h in subs:
            @pl.loop(0, zn)
            def _(k):
                s = lax.rem(z + k, zn)
                pl.when(jnp.logical_not(jnp.logical_and(hub, s == z)))(lambda: fwd(ph, s, h).wait_recv())
                pl.when(direct)(lambda: fwd(ph, s, h).start())
                if h == SUBS - 1:
                    wv[pl.ds(pl.multiple_of(s * pr, pr), pr), :] = split(xv[ph, s])

    def spread_end(ph):
        for h in subs:
            for n in range(1, nx):
                up(ph, n, h).wait_send()
            pl.when(jnp.logical_not(hub))(lambda: up(ph, 0, h).wait_send())
            pl.when(direct)(lambda: pl.loop(0, zn)(lambda s: fwd(ph, s, h).wait_send()))

    def at_out(b, yy, zz, h):
        return piece(out, b, yy, zz).at[sub[h]]

    def dz_copy(b, ph, k, h, zz):
        return remote(tv.at[ph, sub[h]], at_out(b, y, zz, h), d_s.at[b, k, h], d_r.at[b, k, h], dev(zfwd(k), y, i))

    def dy_copy(b, m, slot, s, h, yy):
        return remote(at_out(b, y, s, h), at_out(b, yy, s, h), dy_s.at[b, m, slot, h], dy_r.at[b, m, slot, h],
                      dev(z, yfwd(m), i))

    def publish_z(b, ph, h):
        at_out(b, y, z, h)[...] = tv[ph, sub[h]]
        for k in range(zn - 1):
            dz_copy(b, ph, k, h, z).start()
        for m in range(q - 1):
            dy_copy(b, m, 0, z, h, y).start()

    def publish_y(b, ph, h):
        for k in range(zn - 1):
            dz_copy(b, ph, k, h, zback(k)).wait_recv()
            for m in range(q - 1):
                dy_copy(b, m, k + 1, zback(k), h, y).start()

    def publish_end(b, ph):
        for h in subs:
            for slot in range(zn):
                s = z if slot == 0 else zback(slot - 1)
                for m in range(q - 1):
                    dy_copy(b, m, slot, s, h, yback(m)).wait_recv()
                    dy_copy(b, m, slot, s, h, y).wait_send()
            for k in range(zn - 1):
                dz_copy(b, ph, k, h, z).wait_send()

    def second_carried():
        for m in range(q):
            @pl.loop(0, zn)
            def _(k):
                load(panel.at[1], pbuf, psem, m, k).wait()
                part1[yfwd(m), zfwd(k)] = product(pbuf, w0, m, k)

    reduce(0, panel.at[0], pbuf, psem, w0, False, 0, rise, after=panel.at[1])
    second_carried()
    load_all(coup, buf1, sem1)
    spread(0)
    drain(0, False)
    reduce(1, inv.at[0], buf0, sem0, wv, True, None, rise, after=inv.at[1])
    spread(1)
    drain(1, True)
    for h in subs:
        publish_z(0, 1, h)
    reduce(2, coup, buf1, sem1, wv, False, 1, rise, add=True)
    for h in subs:
        publish_y(0, 1, h)
    spread(2)
    drain(2, False)
    reduce(3, inv.at[1], buf0, sem0, wv, True, None, lambda ph, h: publish_z(1, ph, h))
    for h in subs:
        publish_y(1, 3, h)
    drain(3, True)
    for ph in range(3):
        spread_end(ph)
    publish_end(0, 1)
    publish_end(1, 3)


def shards(nc, nr, panel, prior, right_side, coupling, inverses):
    q = nc // nr
    rows, width = coupling.shape
    r = prior.shape[1]
    pr = rows // nc
    dense = pr % 128 == 0
    lanes = 2 * r
    dma = pltpu.SemaphoreType.DMA
    hbm = pl.BlockSpec(memory_space=pl.ANY)
    vmem = pl.BlockSpec(memory_space=pltpu.VMEM)
    side = right_side.transpose(0, 2, 1)
    if not dense:
        side = side.reshape(2, r, nc, pr).transpose(0, 2, 1, 3)
    solved = pl.pallas_call(
        functools.partial(kernel, q, nr),
        out_shape=jax.ShapeDtypeStruct(side.shape, F32),
        in_specs=[hbm, vmem, hbm, hbm, hbm],
        out_specs=vmem,
        scratch_shapes=[
            pltpu.VMEM((q, nr, r, pr), F32),
            pltpu.VMEM((q, nr, r, pr), F32),
            pltpu.VMEM((4, q - 1, nr, r, pr), F32),
            pltpu.VMEM((4, nr - 1, r, pr), F32),
            pltpu.VMEM((4, r, pr), F32),
            pltpu.VMEM((3, nr, r, pr), F32),
            pltpu.VMEM((width, lanes), BF16),
            pltpu.VMEM((prior.shape[0], lanes), BF16),
            pltpu.VMEM(panel.shape[1:], F32),
            pltpu.VMEM((rows, width), F32),
            pltpu.VMEM((rows, width), F32),
            pltpu.VMEM((2, r, pr), F32),
            dma((nc,)), dma((nc,)), dma((nc,)), dma((2,)),
            dma((4, q - 1, nr, SUBS)), dma((4, q - 1, nr, SUBS)),
            dma((4, nr - 1, SUBS)), dma((4, nr - 1, SUBS)),
            dma((3, nr // 2, SUBS)), dma((3, nr, SUBS)), dma((3, nr, SUBS)),
            dma((2, nr - 1, SUBS)), dma((2, nr - 1, SUBS)),
            dma((2, q - 1, nr, SUBS)), dma((2, q - 1, nr, SUBS)),
        ],
        compiler_params=pltpu.CompilerParams(collective_id=0, has_side_effects=True, vmem_limit_bytes=67043328),
    )(panel, prior.T, side, coupling, inverses)
    if not dense:
        solved = solved.transpose(0, 2, 1, 3).reshape(2, r, rows)
    return solved.transpose(0, 2, 1)


def solution(mesh):
    in_specs = (
        P(None, "row", "col"),
        P("col", None),
        P(None, "row", None),
        P("row", "col"),
        P(None, "row", "col"),
    )
    out_specs = P(None, "row", None)
    body = functools.partial(shards, mesh.shape["col"], mesh.shape["row"])
    return jax.shard_map(body, mesh=mesh, in_specs=in_specs, out_specs=out_specs, check_vma=False)
```

```python
import functools
import jax
import jax.numpy as jnp
from jax import lax
from jax.experimental import pallas as pl
from jax.experimental.pallas import tpu as pltpu
from jax.sharding import PartitionSpec as P

F32, BF16 = jnp.float32, jnp.bfloat16
SUBS = 2


def kernel(q, nr, panel, prior, rs, coup, inv, out, part, part1, ra, rb, tv, xv, wv, w0, pbuf, buf0, buf1, rsv,
           psem, sem0, sem1, rsem, a_s, a_r, b_s, b_r, c1_s, x_r, c2_s, d_s, d_r, dy_s, dy_r):
    zn = nr
    nx = nr // 2
    r, pr = part.shape[2:]
    subs = range(SUBS)
    sub = [pl.ds(h * (r // SUBS), r // SUBS) for h in subs]
    col = lax.axis_index("col")
    i = lax.axis_index("row")
    z, y = lax.div(col, q), lax.rem(col, q)
    below = z <= i
    hub = z == i
    direct = lax.rem(i, 2) == lax.rem(z, 2)
    far = jnp.logical_and(direct, jnp.logical_not(hub))
    sibling = i + 1 - 2 * lax.rem(i, 2)

    def dev(zz, yy, ii):
        return {"col": zz * q + yy, "row": ii}

    def zfwd(k):
        return lax.rem(z + 1 + k, zn)

    def zback(k):
        return lax.rem(z + zn - 1 - k, zn)

    def yfwd(m):
        return lax.rem(y + 1 + m, q)

    def yback(m):
        return lax.rem(y + q - 1 - m, q)

    def remote(src, dst, ss, rr, to):
        return pltpu.make_async_remote_copy(
            src_ref=src, dst_ref=dst, send_sem=ss, recv_sem=rr, device_id=to, device_id_type=pl.DeviceIdType.MESH)

    def rows_of(m, k):
        return pl.ds(pl.multiple_of((yfwd(m) * zn + zfwd(k)) * pr, pr), pr)

    def load(src, dst, sem, m, k):
        rows = rows_of(m, k)
        return pltpu.make_async_copy(src.at[rows, :], dst.at[rows, :], sem.at[m * zn + k])

    def load_all(src, dst, sem):
        for m in range(q):
            pl.loop(0, zn)(lambda k, m=m: load(src, dst, sem, m, k).start())

    load_all(panel.at[0], pbuf, psem)

    def piece(ref, b, yy, zz):
        if len(ref.shape) == 4:
            return ref.at[b, yy * zn + zz]
        return ref.at[b, :, pl.ds(pl.multiple_of((yy * zn + zz) * pr, pr), pr)]

    rs_copies = [pltpu.make_async_copy(piece(rs, b, y, z), rsv.at[b], rsem.at[b]) for b in range(2)]
    for c in rs_copies:
        c.start()
    pl.when(below)(lambda: load_all(inv.at[0], buf0, sem0))

    barrier = pltpu.get_barrier_semaphore()
    for k in range(zn - 1):
        pl.semaphore_signal(barrier, inc=1, device_id=dev(zfwd(k), y, i), device_id_type=pl.DeviceIdType.MESH)
    for m in range(q - 1):
        pl.semaphore_signal(barrier, inc=1, device_id=dev(z, yfwd(m), i), device_id_type=pl.DeviceIdType.MESH)
    for n in range(nr - 1):
        pl.semaphore_signal(barrier, inc=1, device_id=dev(z, y, lax.rem(i + 1 + n, nr)), device_id_type=pl.DeviceIdType.MESH)

    @pl.when(far)
    def _():
        for k in range(zn):
            pl.semaphore_signal(barrier, inc=1, device_id=dev(k, y, z), device_id_type=pl.DeviceIdType.MESH)

    def split(x):
        high = x.astype(BF16).astype(F32)
        return jnp.concatenate([high, x - high], axis=0).T.astype(BF16)

    w0[...] = split(prior[...])
    for c in rs_copies:
        c.wait()
    pl.semaphore_wait(barrier, zn - 1 + q - 1 + nr - 1 + nx - 1)

    def product(buf, w, m, k):
        a = buf[rows_of(m, k), :]
        a1 = a.astype(BF16)
        a2 = (a - a1.astype(F32)).astype(BF16)
        p = jnp.dot(jnp.concatenate([a1, a2], axis=0), w[...], preferred_element_type=F32)
        s = (p[:pr] + p[pr:]).T
        return s[:r] + s[r:]

    def a_copy(ph, m, k, h):
        return remote(part.at[yfwd(m), zfwd(k), sub[h]], ra.at[ph, m, k, sub[h]], a_s.at[ph, m, k, h],
                      a_r.at[ph, m, k, h], dev(z, yfwd(m), i))

    def b_copy(ph, k, h):
        return remote(part.at[y, zfwd(k), sub[h]], rb.at[ph, k, sub[h]], b_s.at[ph, k, h], b_r.at[ph, k, h],
                      dev(zfwd(k), y, i))

    def guard(tri, cond, f):
        if tri:
            pl.when(cond)(f)
        else:
            f()

    def reduce(ph, src, buf, sem, w, tri, rhs, emit, add=False, after=None):
        def absorb(k, h):
            val = part[y, zfwd(k), sub[h]]
            for m in range(q - 1):
                a_copy(ph, m, k, h).wait_recv()
                val = val + ra[ph, m, k, sub[h]]
            part[y, zfwd(k), sub[h]] = val
            pl.when(k < zn - 1)(lambda: b_copy(ph, k, h).start())

        def compute():
            for m in range(q):
                @pl.loop(0, zn)
                def _(k):
                    load(src, buf, sem, m, k).wait()
                    val = product(buf, w, m, k)
                    if add:
                        val = val + part1[yfwd(m), zfwd(k)]
                    part[yfwd(m), zfwd(k)] = val
                    if after is not None:
                        load(after, buf, sem, m, k).start()
                    if m < q - 1:
                        a_copy(ph, m, k, 0).start()
                    else:
                        absorb(k, 0)

                if m < q - 1:
                    for h in subs[1:]:
                        pl.loop(0, zn)(lambda k, m=m, h=h: a_copy(ph, m, k, h).start())
            for h in subs[1:]:
                pl.loop(0, zn)(lambda k, h=h: absorb(k, h))

        guard(tri, below, compute)
        if tri:
            @pl.when(jnp.logical_not(below))
            def _():
                part[y, z] = jnp.zeros((r, pr), F32)
        for h in subs:
            for k in range(zn - 1):
                def take(k=k):
                    b_copy(ph, k, h).wait_recv()
                    part[y, z, sub[h]] = part[y, z, sub[h]] + rb[ph, k, sub[h]]

                guard(tri, zback(k) <= i, take)
            val = part[y, z, sub[h]]
            tv[ph, sub[h]] = val if rhs is None else rsv[rhs, sub[h]] - val
            emit(ph, h)

    def drain(ph, tri):
        def waits():
            for h in subs:
                for m in range(q - 1):
                    pl.loop(0, zn)(lambda k, m=m: a_copy(ph, m, k, h).wait_send())
                pl.loop(0, zn - 1)(lambda k: b_copy(ph, k, h).wait_send())

        guard(tri, below, waits)

    def up(ph, n, h):
        return remote(tv.at[ph, sub[h]], xv.at[ph, z, sub[h]], c1_s.at[ph, n, h], x_r.at[ph, z, h],
                      dev(i, y, lax.rem(i + 2 * n, nr)))

    def fwd(ph, s, h):
        there = xv.at[ph, s, sub[h]]
        return remote(there, there, c2_s.at[ph, s, h], x_r.at[ph, s, h], dev(z, y, sibling))

    def rise(ph, h):
        @pl.when(hub)
        def _():
            xv[ph, z, sub[h]] = tv[ph, sub[h]]

        for n in range(1, nx):
            up(ph, n, h).start()
        pl.when(jnp.logical_not(hub))(lambda: up(ph, 0, h).start())

    def spread(ph):
        for h in subs:
            @pl.loop(0, zn)
            def _(k):
                s = lax.rem(z + k, zn)
                pl.when(jnp.logical_not(jnp.logical_and(hub, s == z)))(lambda: fwd(ph, s, h).wait_recv())
                pl.when(direct)(lambda: fwd(ph, s, h).start())
                if h == SUBS - 1:
                    wv[pl.ds(pl.multiple_of(s * pr, pr), pr), :] = split(xv[ph, s])

    def spread_end(ph):
        for h in subs:
            for n in range(1, nx):
                up(ph, n, h).wait_send()
            pl.when(jnp.logical_not(hub))(lambda: up(ph, 0, h).wait_send())
            pl.when(direct)(lambda: pl.loop(0, zn)(lambda s: fwd(ph, s, h).wait_send()))

    def at_out(b, yy, zz, h):
        return piece(out, b, yy, zz).at[sub[h]]

    def dz_copy(b, ph, k, h, zz):
        return remote(tv.at[ph, sub[h]], at_out(b, y, zz, h), d_s.at[b, k, h], d_r.at[b, k, h], dev(zfwd(k), y, i))

    def dy_copy(b, m, slot, s, h, yy):
        return remote(at_out(b, y, s, h), at_out(b, yy, s, h), dy_s.at[b, m, slot, h], dy_r.at[b, m, slot, h],
                      dev(z, yfwd(m), i))

    def publish_z(b, ph, h):
        at_out(b, y, z, h)[...] = tv[ph, sub[h]]
        for k in range(zn - 1):
            dz_copy(b, ph, k, h, z).start()

    def publish_own(b, h):
        for m in range(q - 1):
            dy_copy(b, m, 0, z, h, y).start()

    def publish_y(b, ph, h):
        for k in range(zn - 1):
            dz_copy(b, ph, k, h, zback(k)).wait_recv()
            for m in range(q - 1):
                dy_copy(b, m, k + 1, zback(k), h, y).start()

    def publish_end(b, ph):
        for h in subs:
            for slot in range(zn):
                s = z if slot == 0 else zback(slot - 1)
                for m in range(q - 1):
                    dy_copy(b, m, slot, s, h, yback(m)).wait_recv()
                    dy_copy(b, m, slot, s, h, y).wait_send()
            for k in range(zn - 1):
                dz_copy(b, ph, k, h, z).wait_send()

    def second_carried():
        for m in range(q):
            @pl.loop(0, zn)
            def _(k):
                load(panel.at[1], pbuf, psem, m, k).wait()
                part1[yfwd(m), zfwd(k)] = product(pbuf, w0, m, k)

    def last(ph, h):
        publish_z(1, ph, h)
        publish_own(1, h)

    reduce(0, panel.at[0], pbuf, psem, w0, False, 0, rise, after=panel.at[1])
    second_carried()
    load_all(coup, buf1, sem1)
    spread(0)
    drain(0, False)
    reduce(1, inv.at[0], buf0, sem0, wv, True, None, rise, after=inv.at[1])
    spread(1)
    drain(1, True)
    publish_z(0, 1, 0)
    reduce(2, coup, buf1, sem1, wv, False, 1, rise, add=True)
    publish_own(0, 0)
    publish_y(0, 1, 0)
    spread(2)
    drain(2, False)
    for h in subs[1:]:
        publish_z(0, 1, h)
        publish_own(0, h)
    reduce(3, inv.at[1], buf0, sem0, wv, True, None, last)
    for h in subs[1:]:
        publish_y(0, 1, h)
    for h in subs:
        publish_y(1, 3, h)
    drain(3, True)
    for ph in range(3):
        spread_end(ph)
    publish_end(0, 1)
    publish_end(1, 3)


def shards(nc, nr, panel, prior, right_side, coupling, inverses):
    q = nc // nr
    rows, width = coupling.shape
    r = prior.shape[1]
    pr = rows // nc
    dense = pr % 128 == 0
    lanes = 2 * r
    dma = pltpu.SemaphoreType.DMA
    hbm = pl.BlockSpec(memory_space=pl.ANY)
    vmem = pl.BlockSpec(memory_space=pltpu.VMEM)
    side = right_side.transpose(0, 2, 1)
    if not dense:
        side = side.reshape(2, r, nc, pr).transpose(0, 2, 1, 3)
    solved = pl.pallas_call(
        functools.partial(kernel, q, nr),
        out_shape=jax.ShapeDtypeStruct(side.shape, F32),
        in_specs=[hbm, vmem, hbm, hbm, hbm],
        out_specs=vmem,
        scratch_shapes=[
            pltpu.VMEM((q, nr, r, pr), F32),
            pltpu.VMEM((q, nr, r, pr), F32),
            pltpu.VMEM((4, q - 1, nr, r, pr), F32),
            pltpu.VMEM((4, nr - 1, r, pr), F32),
            pltpu.VMEM((4, r, pr), F32),
            pltpu.VMEM((3, nr, r, pr), F32),
            pltpu.VMEM((width, lanes), BF16),
            pltpu.VMEM((prior.shape[0], lanes), BF16),
            pltpu.VMEM(panel.shape[1:], F32),
            pltpu.VMEM((rows, width), F32),
            pltpu.VMEM((rows, width), F32),
            pltpu.VMEM((2, r, pr), F32),
            dma((nc,)), dma((nc,)), dma((nc,)), dma((2,)),
            dma((4, q - 1, nr, SUBS)), dma((4, q - 1, nr, SUBS)),
            dma((4, nr - 1, SUBS)), dma((4, nr - 1, SUBS)),
            dma((3, nr // 2, SUBS)), dma((3, nr, SUBS)), dma((3, nr, SUBS)),
            dma((2, nr - 1, SUBS)), dma((2, nr - 1, SUBS)),
            dma((2, q - 1, nr, SUBS)), dma((2, q - 1, nr, SUBS)),
        ],
        compiler_params=pltpu.CompilerParams(collective_id=0, has_side_effects=True, vmem_limit_bytes=67043328),
    )(panel, prior.T, side, coupling, inverses)
    if not dense:
        solved = solved.transpose(0, 2, 1, 3).reshape(2, r, rows)
    return solved.transpose(0, 2, 1)


def solution(mesh):
    in_specs = (
        P(None, "row", "col"),
        P("col", None),
        P(None, "row", None),
        P("row", "col"),
        P(None, "row", "col"),
    )
    out_specs = P(None, "row", None)
    body = functools.partial(shards, mesh.shape["col"], mesh.shape["row"])
    return jax.shard_map(body, mesh=mesh, in_specs=in_specs, out_specs=out_specs, check_vma=False)
```
